256 devices in a mesh: row: 16 (over z_lo, y), col: 16 (over z_hi, x, core).
Axes of the slice: x: 4, y: 4, z: 8 (z_hi: 2, z_lo: 4; z = z_hi * 4 + z_lo), core: 2. Of those that a mesh axis runs over, the one named last changes fastest.
Arguments:
- lambda_amps: float32 [256, 32768], P('col', 'row'), may hold values from -6 to 6
- cycle_inter: float32 [32768, 4096], P('row', 'col'), may hold values from -0.03125 to 0.03125
- exchanged: int32 [4096], replicated, may hold values from 0 to 4095, each once
- occ_energy: float32 [64], replicated, may hold values from -1 to -0.25
- virt_energy: float32 [512], replicated, may hold values from 0.25 to 1.5
- row_orbitals: int32 [256, 2], replicated, may hold values from 0 to 63
- col_orbitals: int32 [4096, 2], replicated, may hold values from 0 to 511
Outputs:
- update: float32 [256, 4096], P(('row', 'col'))
The draws below stay inside these ranges and needn't reach their ends.
All inputs are finite; a program needn't handle non-finite values.
Results may differ from the reference program's by a relative error of at most 0.000088.
Values sent between devices are 32-bit elements; how exact they have to be, the bound alone decides.
No kernel may reach another device: no remote copies, remote signals or barrier semaphores. Data moves between devices by JAX's collectives and lax.ppermute only.
A program may use at most 64 MiB of HBM per device.

```python
import jax
import jax.numpy as jnp
from jax import lax

OCC = 64
VIRT = 512
PAIRS = 32768
WINDOW = 4096
BRA_ROWS = 256


def set_ends(entries, stream_key, low, largest):
    longest = entries.shape.index(max(entries.shape))
    spots = []
    for shift in (0, 1):
        where = [jax.random.randint(jax.random.fold_in(stream_key, axis), (), 0, length) for axis, length in enumerate(entries.shape)]
        where[longest] = (where[longest] + shift) % entries.shape[longest]
        spots.append(tuple(where))
    return entries.at[spots[0]].set(low).at[spots[1]].set(largest)


def steps_of(stream_key, extent, cuts, low, high):
    factor_of = 1.0
    for position, parts in cuts:
        steps = jax.random.uniform(jax.random.fold_in(jax.random.fold_in(stream_key, 6), position), (parts,), jnp.float32, low / len(cuts), high / len(cuts))
        factor_of = factor_of * jnp.repeat(jnp.exp(steps), extent[position] // parts).reshape((-1,) + (1,) * (len(extent) - 1 - position))
    return factor_of


def normal_values(stream_key, extent, width, reach, cuts=(), kind=jnp.bfloat16):
    result = jax.random.normal(stream_key, extent, jnp.float32) * width
    if len(cuts) > 0:
        result = steps_of(stream_key, extent, cuts, -0.22, 0.18) * result
    return jnp.clip(result, min=-reach, max=reach).astype(kind)


def setup_inputs(seed: int = 0) -> dict:
    key_of = jax.random.split(jax.random.key(seed), 8)
    return {
        "lambda_amps": normal_values(key_of[0], (BRA_ROWS, PAIRS), 1.0, 6.0, ((0, 16), (1, 16)), jnp.float32),
        "cycle_inter": normal_values(key_of[1], (PAIRS, WINDOW), PAIRS ** -0.5, 0.03125, ((0, 16), (1, 16)), jnp.float32),
        "exchanged": jax.random.permutation(key_of[2], WINDOW).astype(jnp.int32),
        "occ_energy": jnp.clip(jax.random.uniform(key_of[3], (OCC,), jnp.float32, -1.0, -0.25), -1.0, -0.25),
        "virt_energy": jnp.clip(jax.random.uniform(key_of[4], (VIRT,), jnp.float32, 0.25, 1.5), 0.25, 1.5),
        "row_orbitals": set_ends(jax.random.randint(key_of[5], (BRA_ROWS, 2), 0, OCC), jax.random.fold_in(key_of[5], 1), 0, OCC - 1).astype(jnp.int32),
        "col_orbitals": set_ends(jax.random.randint(key_of[6], (WINDOW, 2), 0, VIRT), jax.random.fold_in(key_of[6], 1), 0, VIRT - 1).astype(jnp.int32),
    }


def reference(lambda_amps, cycle_inter, exchanged, occ_energy, virt_energy, row_orbitals, col_orbitals):
    cycle = jnp.dot(lambda_amps, cycle_inter, precision=lax.Precision.HIGHEST, preferred_element_type=jnp.float32)
    anti = cycle - jnp.take(cycle, exchanged, axis=1)
    row_part = jnp.take(occ_energy, row_orbitals[:, 0]) + jnp.take(occ_energy, row_orbitals[:, 1])
    col_part = jnp.take(virt_energy, col_orbitals[:, 0]) + jnp.take(virt_energy, col_orbitals[:, 1])
    denom = row_part[:, None] - col_part[None, :]
    return anti / denom
```

```python
import functools

import jax
import jax.numpy as jnp
from jax import lax
from jax.experimental import pallas as pl
from jax.experimental.pallas import tpu as pltpu
from jax.sharding import PartitionSpec as P

X, CORES, LANES = 4, 2, 128
VMEM = pltpu.VMEM
SMEM = pltpu.SMEM


def place(z, x, core):
    return (z * X + x % X) * CORES + core


def shift(dz=0, dx=0, dcore=0):
    return [
        (place(z, x, core), place(z ^ dz, x + dx, core ^ dcore))
        for z in range(2)
        for x in range(X)
        for core in range(CORES)
    ]


def lookup(table, where):
    row, lane = where // LANES, where % LANES
    found = jnp.zeros(where.shape, table.dtype)
    for k in range(table.shape[0]):
        line = jnp.broadcast_to(table[k : k + 1], where.shape)
        line = jnp.take_along_axis(line, lane, axis=1, mode="promise_in_bounds")
        found = jnp.where(row == k, line, found)
    return found


def denominators(virt_ref, col_ref, occ_ref, row_ref, out_ref):
    me = lax.axis_index("row") * lax.axis_size("col") + lax.axis_index("col")
    row_part = occ_ref[row_ref[0, me]] + occ_ref[row_ref[1, me]]
    for k in range(0, out_ref.shape[0], 8):
        first = lookup(virt_ref[...], col_ref[0, k : k + 8])
        second = lookup(virt_ref[...], col_ref[1, k : k + 8])
        out_ref[k : k + 8] = row_part - (first + second)


def halves(value):
    high = value.astype(jnp.bfloat16)
    return high, (value - high.astype(jnp.float32)).astype(jnp.bfloat16)


def product(block_refs, b_ref, a_ref):
    rows = block_refs[0].shape[0]
    total = rows * len(block_refs)
    for k, block in enumerate(block_refs):
        high, low = halves(block[...])
        a_ref[k * rows : (k + 1) * rows] = high
        a_ref[total + k * rows : total + (k + 1) * rows] = low
    b_high, b_low = halves(b_ref[...])
    both = jnp.dot(a_ref[...], b_high, preferred_element_type=jnp.float32)
    rest = jnp.dot(a_ref[:total], b_low, preferred_element_type=jnp.float32)
    return both[:total] + (both[total:] + rest)


def near(*refs):
    *blocks, b_ref, out_ref, a_ref = refs
    out_ref[...] = product(blocks, b_ref, a_ref)


def far(*refs):
    *blocks, b_ref, near_ref, out_ref, a_ref, done_ref = refs
    rows = blocks[0].shape[0]
    done_ref[...] = product(blocks, b_ref, a_ref)
    me = lax.axis_index("col")
    z, x, core = me // (X * CORES), (me // CORES) % X, me % CORES
    for ref, dz in ((near_ref, 0), (done_ref, 1)):
        for k in range(len(blocks)):
            source = place(z ^ dz, x + X - k % X, core ^ (k // X))
            for h in range(2):
                out_ref[pl.ds(source * (2 * rows) + h, rows, stride=2), :] = ref[
                    k * rows : (k + 1) * rows, h * LANES : (h + 1) * LANES
                ]


def finish(parts_ref, exchanged_ref, denom_ref, out_ref, cycle_ref):
    lines = out_ref.shape[0]
    total = parts_ref[:lines]
    for k in range(1, parts_ref.shape[0] // lines):
        total = total + parts_ref[k * lines : (k + 1) * lines]
    cycle_ref[...] = total
    for k in range(0, lines, 8):
        other = lookup(cycle_ref[...], exchanged_ref[k : k + 8])
        out_ref[k : k + 8] = (cycle_ref[k : k + 8] - other) / denom_ref[k : k + 8]


def shards(
    lambda_amps, cycle_inter, exchanged, occ_energy, virt_energy, row_orbitals, col_orbitals
):
    rows, depth = lambda_amps.shape
    window = exchanged.shape[0]
    width = cycle_inter.shape[1]
    lines = window // LANES
    f32 = functools.partial(jax.ShapeDtypeStruct, dtype=jnp.float32)
    v, s = pl.BlockSpec(memory_space=VMEM), pl.BlockSpec(memory_space=SMEM)

    def spread(block):
        line = [block] + [lax.ppermute(block, "col", shift(dx=k)) for k in (1, 2, 3)]
        return line + [lax.ppermute(part, "col", shift(dcore=1)) for part in line]

    swapped = lax.ppermute(lambda_amps, "col", shift(dz=1))
    near_blocks = spread(lambda_amps)
    denom = pl.pallas_call(
        denominators,
        out_shape=f32((lines, LANES)),
        in_specs=[v, v, s, s],
        out_specs=v,
    )(
        virt_energy.reshape(-1, LANES),
        col_orbitals.T.reshape(2, lines, LANES),
        occ_energy,
        row_orbitals.T,
    )
    count = len(near_blocks)
    split = pltpu.VMEM((2 * count * rows, depth), jnp.bfloat16)
    near_part = pl.pallas_call(
        near,
        out_shape=f32((count * rows, width)),
        in_specs=[v] * (count + 1),
        out_specs=v,
        scratch_shapes=[split],
    )(*near_blocks, cycle_inter)
    far_blocks = spread(swapped)
    parts = pl.pallas_call(
        far,
        out_shape=f32((4 * count * rows, LANES)),
        in_specs=[v] * (count + 2),
        out_specs=v,
        scratch_shapes=[split, pltpu.VMEM((count * rows, width), jnp.float32)],
    )(*far_blocks, cycle_inter, near_part)
    owners = lax.axis_size("row") * lax.axis_size("col")
    parts = lax.all_to_all(
        parts.reshape(owners, -1, LANES), ("row", "col"), 0, 0, tiled=True
    )
    update = pl.pallas_call(
        finish,
        out_shape=f32((lines, LANES)),
        in_specs=[v, v, v],
        out_specs=v,
        scratch_shapes=[pltpu.VMEM((lines, LANES), jnp.float32)],
    )(parts.reshape(-1, LANES), exchanged.reshape(lines, LANES), denom)
    return update.reshape(1, window)


def solution(mesh):
    placed = (P("col", "row"), P("row", "col"), P(), P(), P(), P(), P())
    return jax.shard_map(
        shards, mesh=mesh, in_specs=placed, out_specs=P(("row", "col"), None), check_vma=False
    )
```

```python
import jax
import jax.numpy as jnp
from jax import lax
from jax.experimental import pallas as pl
from jax.experimental.pallas import tpu as pltpu
from jax.sharding import PartitionSpec as P

X, CORES, LANES = 4, 2, 128
VMEM = pltpu.VMEM
SMEM = pltpu.SMEM
LIMIT = pltpu.CompilerParams(vmem_limit_bytes=24 << 20)


def place(z, x, core):
    return (z * X + x % X) * CORES + core


def shift(dz=0, dx=0, dcore=0):
    return [
        (place(z, x, core), place(z ^ dz, x + dx, core ^ dcore))
        for z in range(2)
        for x in range(X)
        for core in range(CORES)
    ]


def lookup(table, where):
    row, lane = where // LANES, where % LANES
    found = jnp.zeros(where.shape, table.dtype)
    for k in range(table.shape[0]):
        line = jnp.broadcast_to(table[k : k + 1], where.shape)
        line = jnp.take_along_axis(line, lane, axis=1, mode="promise_in_bounds")
        found = jnp.where(row == k, line, found)
    return found


def halves(value):
    high = value.astype(jnp.bfloat16)
    return high, (value - high.astype(jnp.float32)).astype(jnp.bfloat16)


def prepare(virt_ref, col_ref, occ_ref, row_ref, b_ref, denom_ref, high_ref, low_ref):
    high_ref[...], low_ref[...] = halves(b_ref[...])
    me = lax.axis_index("row") * lax.axis_size("col") + lax.axis_index("col")
    row_part = occ_ref[row_ref[0, me]] + occ_ref[row_ref[1, me]]
    for k in range(denom_ref.shape[0]):
        lanes = slice(k * LANES, (k + 1) * LANES)
        pair = lookup(virt_ref[...], col_ref[:, lanes])
        denom_ref[k : k + 1] = row_part - (pair[:1] + pair[1:])


def product(block_refs, high_ref, low_ref, a_ref):
    rows = block_refs[0].shape[0]
    total = rows * len(block_refs)
    for k, block in enumerate(block_refs):
        high, low = halves(block[...])
        a_ref[k * rows : (k + 1) * rows] = high
        a_ref[total + k * rows : total + (k + 1) * rows] = low
    both = jnp.dot(a_ref[...], high_ref[...], preferred_element_type=jnp.float32)
    rest = jnp.dot(a_ref[:total], low_ref[...], preferred_element_type=jnp.float32)
    return both[:total] + (both[total:] + rest)


def near(*refs):
    *blocks, high_ref, low_ref, out_ref, a_ref = refs
    out_ref[...] = product(blocks, high_ref, low_ref, a_ref)


def far(*refs):
    *blocks, high_ref, low_ref, near_ref, out_ref, a_ref, done_ref = refs
    rows = blocks[0].shape[0]
    done_ref[...] = product(blocks, high_ref, low_ref, a_ref)
    me = lax.axis_index("col")
    z, x, core = me // (X * CORES), (me // CORES) % X, me % CORES
    for ref, dz in ((near_ref, 0), (done_ref, 1)):
        for k in range(len(blocks)):
            source = place(z ^ dz, x + X - k % X, core ^ (k // X))
            for h in range(2):
                out_ref[pl.ds(source * (2 * rows) + h, rows, stride=2), :] = ref[
                    k * rows : (k + 1) * rows, h * LANES : (h + 1) * LANES
                ]


def finish(parts_ref, exchanged_ref, denom_ref, out_ref, cycle_ref):
    lines = out_ref.shape[0]
    total = parts_ref[:lines]
    for k in range(1, parts_ref.shape[0] // lines):
        total = total + parts_ref[k * lines : (k + 1) * lines]
    cycle_ref[...] = total
    for k in range(0, lines, 8):
        other = lookup(cycle_ref[...], exchanged_ref[k : k + 8])
        out_ref[k : k + 8] = (cycle_ref[k : k + 8] - other) / denom_ref[k : k + 8]


def shards(
    lambda_amps, cycle_inter, exchanged, occ_energy, virt_energy, row_orbitals, col_orbitals
):
    rows, depth = lambda_amps.shape
    window = exchanged.shape[0]
    width = cycle_inter.shape[1]
    lines = window // LANES
    count = X * CORES
    v, s = pl.BlockSpec(memory_space=VMEM), pl.BlockSpec(memory_space=SMEM)
    split = VMEM((2 * count * rows, depth), jnp.bfloat16)

    def here(value):
        return pltpu.with_memory_space_constraint(value, VMEM)

    def send(block, **by):
        return lax.ppermute(block, "col", shift(**by))

    def spread(block):
        line = [block] + [send(block, dx=k) for k in (1, 2, 3)]
        return line + [send(part, dcore=1) for part in line]

    swapped = send(lambda_amps, dz=1)
    near_blocks = spread(lambda_amps)
    denom, high, low = pl.pallas_call(
        prepare,
        out_shape=(
            VMEM((lines, LANES), jnp.float32),
            VMEM(cycle_inter.shape, jnp.bfloat16),
            VMEM(cycle_inter.shape, jnp.bfloat16),
        ),
        in_specs=[v, v, s, s, v],
        out_specs=(v, v, v),
        compiler_params=LIMIT,
    )(
        virt_energy.reshape(-1, LANES),
        col_orbitals.T,
        occ_energy,
        row_orbitals.T,
        here(cycle_inter),
    )
    near_part = pl.pallas_call(
        near,
        out_shape=VMEM((count * rows, width), jnp.float32),
        in_specs=[v] * (count + 2),
        out_specs=v,
        scratch_shapes=[split],
        compiler_params=LIMIT,
    )(*map(here, near_blocks), here(high), here(low))
    far_blocks = spread(swapped)
    parts = pl.pallas_call(
        far,
        out_shape=VMEM((4 * count * rows, LANES), jnp.float32),
        in_specs=[v] * (count + 3),
        out_specs=v,
        scratch_shapes=[split, VMEM((count * rows, width), jnp.float32)],
        compiler_params=LIMIT,
    )(*map(here, far_blocks), here(high), here(low), here(near_part))
    owners = lax.axis_size("row") * lax.axis_size("col")
    parts = lax.all_to_all(
        parts.reshape(owners, -1, LANES), ("row", "col"), 0, 0, tiled=True
    )
    update = pl.pallas_call(
        finish,
        out_shape=jax.ShapeDtypeStruct((lines, LANES), jnp.float32),
        in_specs=[v, v, v],
        out_specs=v,
        scratch_shapes=[VMEM((lines, LANES), jnp.float32)],
        compiler_params=LIMIT,
    )(here(parts.reshape(-1, LANES)), exchanged.reshape(lines, LANES), here(denom))
    return update.reshape(1, window)


def solution(mesh):
    placed = (P("col", "row"), P("row", "col"), P(), P(), P(), P(), P())

    return jax.shard_map(
        shards, mesh=mesh, in_specs=placed, out_specs=P(("row", "col"), None), check_vma=False
    )
```

```python
import jax
import jax.numpy as jnp
from jax import lax
from jax.experimental import pallas as pl
from jax.experimental.pallas import tpu as pltpu
from jax.sharding import PartitionSpec as P

X, CORES, LANES, PIECES = 4, 2, 128, 4
VMEM = pltpu.VMEM
SMEM = pltpu.SMEM
LIMIT = pltpu.CompilerParams(vmem_limit_bytes=24 << 20)


def place(z, x, core):
    return (z * X + x % X) * CORES + core


def position():
    me = lax.axis_index("col")
    return me // (X * CORES), (me // CORES) % X, me % CORES


def shift(dz=0, dx=0, dcore=0):
    return [
        (place(z, x, core), place(z ^ dz, x + dx, core ^ dcore))
        for z in range(2)
        for x in range(X)
        for core in range(CORES)
    ]


def lookup(table, where):
    row, lane = where // LANES, where % LANES
    found = jnp.zeros(where.shape, table.dtype)
    for k in range(table.shape[0]):
        line = jnp.broadcast_to(table[k : k + 1], where.shape)
        line = jnp.take_along_axis(line, lane, axis=1, mode="promise_in_bounds")
        found = jnp.where(row == k, line, found)
    return found


def halves(value):
    high = value.astype(jnp.bfloat16)
    return high, (value - high.astype(jnp.float32)).astype(jnp.bfloat16)


def choose(own_ref, other_ref, out_ref):
    core = position()[2]
    half = own_ref.shape[0] // CORES
    line = lax.broadcasted_iota(jnp.int32, (half, LANES), 0)
    spot = (CORES * line + core) % half
    for ref, at in ((own_ref, core), (other_ref, 1 - core)):
        for k in range(0, ref.shape[1], LANES):
            upper, lower = (
                jnp.take_along_axis(
                    ref[h : h + half, k : k + LANES], spot, axis=0, mode="promise_in_bounds"
                )
                for h in (0, half)
            )
            chosen = jnp.where(line < half // CORES, upper, lower)
            out_ref[pl.ds(pl.multiple_of(at * half, half), half), k : k + LANES] = chosen


def stage(block_ref, out_ref, sem):
    copy = pltpu.make_async_copy(block_ref, out_ref, sem)
    copy.start()
    copy.wait()


def prepare(
    virt_ref, col_ref, occ_ref, row_ref, b_ref, other_ref,
    denom_ref, high_ref, low_ref,
    virt, cols, occ, rows, b, sems, b_sems,
):
    copies = [
        pltpu.make_async_copy(source, target, sems.at[k])
        for k, (source, target) in enumerate(
            ((virt_ref, virt), (col_ref, cols), (occ_ref, occ), (row_ref, rows))
        )
    ]
    step = b.shape[0] // PIECES
    pieces = [pl.ds(k * step, step) for k in range(PIECES)]
    b_copies = [
        pltpu.make_async_copy(b_ref.at[piece], b.at[piece], b_sems.at[k])
        for k, piece in enumerate(pieces)
    ]
    for copy in copies + b_copies:
        copy.start()
    for copy in copies:
        copy.wait()
    me = lax.axis_index("row") * lax.axis_size("col") + lax.axis_index("col")
    row_part = occ[rows[0, me]] + occ[rows[1, me]]
    for k in range(denom_ref.shape[0]):
        pair = lookup(virt[...], cols[:, k * LANES : (k + 1) * LANES])
        denom_ref[k : k + 1] = row_part - (pair[:1] + pair[1:])
    width = b.shape[1]
    for copy, piece in zip(b_copies, pieces):
        copy.wait()
        high_ref[piece, :width], low_ref[piece, :width] = halves(b[piece, :])
    high_ref[:, width:], low_ref[:, width:] = halves(other_ref[...])


def product(block_refs, high_ref, low_ref, a_ref):
    rows = block_refs[0].shape[0]
    total = rows * len(block_refs)
    for k, block in enumerate(block_refs):
        high, low = halves(block[...])
        a_ref[k * rows : (k + 1) * rows] = high
        a_ref[total + k * rows : total + (k + 1) * rows] = low
    both = jnp.dot(a_ref[...], high_ref[...], preferred_element_type=jnp.float32)
    rest = jnp.dot(a_ref[:total], low_ref[...], preferred_element_type=jnp.float32)
    return both[:total] + (both[total:] + rest)


def near(*refs):
    *blocks, high_ref, low_ref, out_ref, a_ref = refs
    out_ref[...] = product(blocks, high_ref, low_ref, a_ref)


def far(*refs):
    *blocks, high_ref, low_ref, near_ref, out_ref, a_ref, done_ref = refs
    rows = blocks[0].shape[0]
    done_ref[...] = product(blocks, high_ref, low_ref, a_ref)
    z, x, core = position()
    each = done_ref.shape[1] // LANES
    for ref, dz in ((near_ref, 0), (done_ref, 1)):
        for k in range(X):
            first = place(z ^ dz, x + X - k, 0) // CORES * (rows * each)
            for q in range(each):
                to = (core ^ (q // (each // CORES))) * (each // CORES) + q % (each // CORES)
                out_ref[pl.ds(first + to, rows, stride=each), :] = ref[
                    k * rows : (k + 1) * rows, q * LANES : (q + 1) * LANES
                ]


def finish(parts_ref, exchanged_ref, denom_ref, out_ref, cycle_ref):
    lines = out_ref.shape[0]
    total = parts_ref[:lines]
    for k in range(1, parts_ref.shape[0] // lines):
        total = total + parts_ref[k * lines : (k + 1) * lines]
    cycle_ref[...] = total
    for k in range(0, lines, 8):
        other = lookup(cycle_ref[...], exchanged_ref[k : k + 8])
        out_ref[k : k + 8] = (cycle_ref[k : k + 8] - other) / denom_ref[k : k + 8]


def shards(
    lambda_amps, cycle_inter, exchanged, occ_energy, virt_energy, row_orbitals, col_orbitals
):
    rows, depth = lambda_amps.shape
    window = exchanged.shape[0]
    wide = (depth, CORES * cycle_inter.shape[1])
    lines = window // LANES
    v, anywhere = pl.BlockSpec(memory_space=VMEM), pl.BlockSpec(memory_space=pl.ANY)
    split = VMEM((2 * X * rows, depth), jnp.bfloat16)
    part = VMEM((X * rows, wide[1]), jnp.float32)

    def here(value):
        return pltpu.with_memory_space_constraint(value, VMEM)

    def send(block, **by):
        return lax.ppermute(block, "col", shift(**by))

    def spread(block, *steps):
        return {k: send(block, dx=k) for k in steps}

    other = send(lambda_amps, dcore=1)
    own = pl.pallas_call(
        stage,
        out_shape=VMEM(lambda_amps.shape, jnp.float32),
        in_specs=[anywhere],
        out_specs=v,
        scratch_shapes=[pltpu.SemaphoreType.DMA],
        compiler_params=LIMIT,
    )(pltpu.with_memory_space_constraint(lambda_amps, pltpu.HBM))
    block = pl.pallas_call(
        choose,
        out_shape=VMEM(lambda_amps.shape, jnp.float32),
        in_specs=[v, v],
        out_specs=v,
        compiler_params=LIMIT,
    )(here(own), here(other))
    swapped = send(block, dz=1)
    other_inter = send(cycle_inter, dcore=1)
    near_blocks = {0: block, **spread(block, 1, 2, 3)}
    denom, high, low = pl.pallas_call(
        prepare,
        out_shape=(
            VMEM((lines, LANES), jnp.float32),
            VMEM(wide, jnp.bfloat16),
            VMEM(wide, jnp.bfloat16),
        ),
        in_specs=[anywhere] * 5 + [v],
        out_specs=(v, v, v),
        scratch_shapes=[
            VMEM((virt_energy.shape[0] // LANES, LANES), jnp.float32),
            VMEM((2, window), jnp.int32),
            SMEM(occ_energy.shape, jnp.float32),
            SMEM((2, row_orbitals.shape[0]), jnp.int32),
            VMEM(cycle_inter.shape, jnp.float32),
            pltpu.SemaphoreType.DMA((4,)),
            pltpu.SemaphoreType.DMA((PIECES,)),
        ],
        compiler_params=LIMIT,
    )(
        *(
            pltpu.with_memory_space_constraint(value, pltpu.HBM)
            for value in (
                virt_energy.reshape(-1, LANES),
                col_orbitals.T,
                occ_energy,
                row_orbitals.T,
                cycle_inter,
            )
        ),
        here(other_inter),
    )
    near_part = pl.pallas_call(
        near,
        out_shape=part,
        in_specs=[v] * (X + 2),
        out_specs=v,
        scratch_shapes=[split],
        compiler_params=LIMIT,
    )(*(here(near_blocks[k]) for k in range(X)), here(high), here(low))
    far_blocks = {0: swapped, **spread(swapped, 1, 2, 3)}
    owners = lax.axis_size("row") * lax.axis_size("col")
    each = wide[1] // LANES
    parts = pl.pallas_call(
        far,
        out_shape=VMEM((owners // CORES * each, LANES), jnp.float32),
        in_specs=[v] * (X + 3),
        out_specs=v,
        scratch_shapes=[split, part],
        compiler_params=LIMIT,
    )(*(here(far_blocks[k]) for k in range(X)), here(high), here(low), here(near_part))
    parts = lax.all_to_all(
        parts.reshape(-1, each, LANES),
        ("row", "col"),
        0,
        0,
        tiled=True,
        axis_index_groups=[list(range(core, owners, CORES)) for core in range(CORES)],
    )
    update = pl.pallas_call(
        finish,
        out_shape=jax.ShapeDtypeStruct((lines, LANES), jnp.float32),
        in_specs=[v, v, v],
        out_specs=v,
        scratch_shapes=[VMEM((lines, LANES), jnp.float32)],
        compiler_params=LIMIT,
    )(here(parts.reshape(-1, LANES)), exchanged.reshape(lines, LANES), here(denom))
    return update.reshape(1, window)


def solution(mesh):
    placed = (P("col", "row"), P("row", "col"), P(), P(), P(), P(), P())

    return jax.shard_map(
        shards, mesh=mesh, in_specs=placed, out_specs=P(("row", "col"), None), check_vma=False
    )
```

```python
import jax
import jax.numpy as jnp
from jax import lax
from jax.experimental import pallas as pl
from jax.experimental.pallas import tpu as pltpu
from jax.sharding import PartitionSpec as P

X, CORES, LANES, PIECES = 4, 2, 128, 4
VMEM = pltpu.VMEM
SMEM = pltpu.SMEM
LIMIT = pltpu.CompilerParams(vmem_limit_bytes=24 << 20)


def place(z, x, core):
    return (z * X + x) * CORES + core


def position():
    me = lax.axis_index("col")
    return me // (X * CORES), (me // CORES) % X, me % CORES


def shift(dz=0, dx=0, dcore=0):
    return [
        (place(z, x, core), place(z ^ dz, x ^ dx, core ^ dcore))
        for z in range(2)
        for x in range(X)
        for core in range(CORES)
    ]


def lookup(table, where):
    row, lane = where // LANES, where % LANES
    found = jnp.zeros(where.shape, table.dtype)
    for k in range(table.shape[0]):
        line = jnp.broadcast_to(table[k : k + 1], where.shape)
        line = jnp.take_along_axis(line, lane, axis=1, mode="promise_in_bounds")
        found = jnp.where(row == k, line, found)
    return found


def halves(value):
    high = value.astype(jnp.bfloat16)
    return high, (value - high.astype(jnp.float32)).astype(jnp.bfloat16)


def choose(own_ref, other_ref, out_ref):
    core = position()[2]
    half = own_ref.shape[0] // CORES
    line = lax.broadcasted_iota(jnp.int32, (half, LANES), 0)
    spot = (CORES * line + core) % half
    for ref, at in ((own_ref, core), (other_ref, 1 - core)):
        for k in range(0, ref.shape[1], LANES):
            upper, lower = (
                jnp.take_along_axis(
                    ref[h : h + half, k : k + LANES], spot, axis=0, mode="promise_in_bounds"
                )
                for h in (0, half)
            )
            chosen = jnp.where(line < half // CORES, upper, lower)
            out_ref[pl.ds(pl.multiple_of(at * half, half), half), k : k + LANES] = chosen


def stage(block_ref, out_ref, sem):
    copy = pltpu.make_async_copy(block_ref, out_ref, sem)
    copy.start()
    copy.wait()


def prepare(
    virt_ref, col_ref, occ_ref, row_ref, b_ref, other_ref,
    denom_ref, high_ref, low_ref,
    virt, cols, occ, rows, b, sems, b_sems,
):
    copies = [
        pltpu.make_async_copy(source, target, sems.at[k])
        for k, (source, target) in enumerate(
            ((virt_ref, virt), (col_ref, cols), (occ_ref, occ), (row_ref, rows))
        )
    ]
    step = b.shape[0] // PIECES
    pieces = [pl.ds(k * step, step) for k in range(PIECES)]
    b_copies = [
        pltpu.make_async_copy(b_ref.at[piece], b.at[piece], b_sems.at[k])
        for k, piece in enumerate(pieces)
    ]
    for copy in copies + b_copies:
        copy.start()
    for copy in copies:
        copy.wait()
    me = lax.axis_index("row") * lax.axis_size("col") + lax.axis_index("col")
    row_part = occ[rows[0, me]] + occ[rows[1, me]]
    for k in range(denom_ref.shape[0]):
        pair = lookup(virt[...], cols[:, k * LANES : (k + 1) * LANES])
        denom_ref[k : k + 1] = row_part - (pair[:1] + pair[1:])
    width = b.shape[1]
    for copy, piece in zip(b_copies, pieces):
        copy.wait()
        high_ref[piece, :width], low_ref[piece, :width] = halves(b[piece, :])
    high_ref[:, width:], low_ref[:, width:] = halves(other_ref[...])


def product(block_refs, high_ref, low_ref, a_ref):
    rows = block_refs[0].shape[0]
    total = rows * len(block_refs)
    for k, block in enumerate(block_refs):
        high, low = halves(block[...])
        a_ref[k * rows : (k + 1) * rows] = high
        a_ref[total + k * rows : total + (k + 1) * rows] = low
    both = jnp.dot(a_ref[...], high_ref[...], preferred_element_type=jnp.float32)
    rest = jnp.dot(a_ref[:total], low_ref[...], preferred_element_type=jnp.float32)
    return both[:total] + (both[total:] + rest)


def near(*refs):
    *blocks, high_ref, low_ref, out_ref, a_ref = refs
    out_ref[...] = product(blocks, high_ref, low_ref, a_ref)


def far(*refs):
    *blocks, high_ref, low_ref, near_ref, out_ref, a_ref, done_ref = refs
    rows = blocks[0].shape[0]
    done_ref[...] = product(blocks, high_ref, low_ref, a_ref)
    z, x, core = position()
    each = done_ref.shape[1] // LANES
    for ref, dz in ((near_ref, 0), (done_ref, 1)):
        for k in range(X):
            first = place(z ^ dz, x ^ k, 0) // CORES * (rows * each)
            for q in range(each):
                to = (core ^ (q // (each // CORES))) * (each // CORES) + q % (each // CORES)
                out_ref[pl.ds(first + to, rows, stride=each), :] = ref[
                    k * rows : (k + 1) * rows, q * LANES : (q + 1) * LANES
                ]


def finish(parts_ref, exchanged_ref, denom_ref, out_ref, cycle_ref):
    lines = out_ref.shape[0]
    total = parts_ref[:lines]
    for k in range(1, parts_ref.shape[0] // lines):
        total = total + parts_ref[k * lines : (k + 1) * lines]
    cycle_ref[...] = total
    for k in range(0, lines, 8):
        other = lookup(cycle_ref[...], exchanged_ref[k : k + 8])
        out_ref[k : k + 8] = (cycle_ref[k : k + 8] - other) / denom_ref[k : k + 8]


def shards(
    lambda_amps, cycle_inter, exchanged, occ_energy, virt_energy, row_orbitals, col_orbitals
):
    rows, depth = lambda_amps.shape
    window = exchanged.shape[0]
    wide = (depth, CORES * cycle_inter.shape[1])
    lines = window // LANES
    v, anywhere = pl.BlockSpec(memory_space=VMEM), pl.BlockSpec(memory_space=pl.ANY)
    split = VMEM((2 * X * rows, depth), jnp.bfloat16)
    part = VMEM((X * rows, wide[1]), jnp.float32)

    def here(value):
        return pltpu.with_memory_space_constraint(value, VMEM)

    def send(block, **by):
        return lax.ppermute(block, "col", shift(**by))

    def spread(block, *steps):
        return {k: send(block, dx=k) for k in steps}

    other = send(lambda_amps, dcore=1)
    own = pl.pallas_call(
        stage,
        out_shape=VMEM(lambda_amps.shape, jnp.float32),
        in_specs=[anywhere],
        out_specs=v,
        scratch_shapes=[pltpu.SemaphoreType.DMA],
        compiler_params=LIMIT,
    )(pltpu.with_memory_space_constraint(lambda_amps, pltpu.HBM))
    block = pl.pallas_call(
        choose,
        out_shape=VMEM(lambda_amps.shape, jnp.float32),
        in_specs=[v, v],
        out_specs=v,
        compiler_params=LIMIT,
    )(here(own), here(other))
    swapped = send(block, dz=1)
    other_inter = send(cycle_inter, dcore=1)
    near_blocks = {0: block, **spread(block, 1, 2, 3)}
    denom, high, low = pl.pallas_call(
        prepare,
        out_shape=(
            VMEM((lines, LANES), jnp.float32),
            VMEM(wide, jnp.bfloat16),
            VMEM(wide, jnp.bfloat16),
        ),
        in_specs=[anywhere] * 5 + [v],
        out_specs=(v, v, v),
        scratch_shapes=[
            VMEM((virt_energy.shape[0] // LANES, LANES), jnp.float32),
            VMEM((2, window), jnp.int32),
            SMEM(occ_energy.shape, jnp.float32),
            SMEM((2, row_orbitals.shape[0]), jnp.int32),
            VMEM(cycle_inter.shape, jnp.float32),
            pltpu.SemaphoreType.DMA((4,)),
            pltpu.SemaphoreType.DMA((PIECES,)),
        ],
        compiler_params=LIMIT,
    )(
        *(
            pltpu.with_memory_space_constraint(value, pltpu.HBM)
            for value in (
                virt_energy.reshape(-1, LANES),
                col_orbitals.T,
                occ_energy,
                row_orbitals.T,
                cycle_inter,
            )
        ),
        here(other_inter),
    )
    near_part = pl.pallas_call(
        near,
        out_shape=part,
        in_specs=[v] * (X + 2),
        out_specs=v,
        scratch_shapes=[split],
        compiler_params=LIMIT,
    )(*(here(near_blocks[k]) for k in range(X)), here(high), here(low))
    far_blocks = {0: swapped, **spread(swapped, 1, 2, 3)}
    owners = lax.axis_size("row") * lax.axis_size("col")
    each = wide[1] // LANES
    parts = pl.pallas_call(
        far,
        out_shape=VMEM((owners // CORES * each, LANES), jnp.float32),
        in_specs=[v] * (X + 3),
        out_specs=v,
        scratch_shapes=[split, part],
        compiler_params=LIMIT,
    )(*(here(far_blocks[k]) for k in range(X)), here(high), here(low), here(near_part))
    parts = lax.all_to_all(
        parts.reshape(-1, 1, each * LANES),
        ("row", "col"),
        0,
        0,
        tiled=True,
        axis_index_groups=[list(range(core, owners, CORES)) for core in range(CORES)],
    )
    update = pl.pallas_call(
        finish,
        out_shape=jax.ShapeDtypeStruct((lines, LANES), jnp.float32),
        in_specs=[v, v, v],
        out_specs=v,
        scratch_shapes=[VMEM((lines, LANES), jnp.float32)],
        compiler_params=LIMIT,
    )(here(parts.reshape(-1, LANES)), exchanged.reshape(lines, LANES), here(denom))
    return update.reshape(1, window)


def solution(mesh):
    placed = (P("col", "row"), P("row", "col"), P(), P(), P(), P(), P())

    return jax.shard_map(
        shards, mesh=mesh, in_specs=placed, out_specs=P(("row", "col"), None), check_vma=False
    )
```
